768 devices in a mesh: section: 96 (over z, y_hi, core), tm: 8 (over y_lo, x).
Axes of the slice: x: 4, y: 8 (y_hi: 4, y_lo: 2; y = y_hi * 2 + y_lo), z: 12, core: 2. Of those that a mesh axis runs over, the one named last changes fastest.
Arguments:
- act_in: bfloat16 [96, 1024, 2048], P('section', 'tm'), may hold values from -6 to 6
- grad_in: bfloat16 [96, 1024, 2048], P('section', 'tm'), may hold values from -6 to 6
- saved_inputs: bfloat16 [96, 2, 1024, 2048], P('section', None, 'tm'), may hold values from -6 to 6
- kernels: bfloat16 [96, 2, 31, 2048], P('section'), may hold values from -1 to 1
- norm_gains: bfloat16 [96, 2, 2048], P('section'), may hold values from 0.099609375 to 1.8984375
- forward_lengths: int32 [96], replicated, may hold values from 512 to 1024
- backward_lengths: int32 [96], replicated, may hold values from 512 to 1024
- forward_slots: int32 [96, 2], replicated, may hold values from 0 to 1
- backward_slots: int32 [96, 2], replicated, may hold values from 0 to 1
Outputs:
- act_out: bfloat16 [96, 1024, 2048], P('section', 'tm')
- grad_out: bfloat16 [96, 1024, 2048], P('section', 'tm')
- tap_grad: float32 [96, 2, 31, 2048], P('section')
- gain_grad: float32 [96, 2, 2048], P('section')
The draws below stay inside these ranges and needn't reach their ends.
All inputs are finite; a program needn't handle non-finite values.
Results may differ from the reference program's by a relative error of at most 0.0063.
Values may be sent and summed in bfloat16 or wider, within the bound.
A program may use at most 32 MiB of HBM per device.

```python
import jax
import jax.numpy as jnp
from jax import lax

D = 2048
KW = 31
RES = 2
TICKS = 2
FRAMES = 1024
SECTIONS = 96


def place_ends(drawn, rng, smallest, high):
    longest = drawn.shape.index(max(drawn.shape))
    spots = []
    for shift in (0, 1):
        where = [jax.random.randint(jax.random.fold_in(rng, axis), (), 0, length) for axis, length in enumerate(drawn.shape)]
        where[longest] = (where[longest] + shift) % drawn.shape[longest]
        spots.append(tuple(where))
    return drawn.at[spots[0]].set(smallest).at[spots[1]].set(high)


def shard_levels(key, dims, cuts, smallest, largest):
    def one(position, shards_of):
        draws = jax.random.uniform(jax.random.fold_in(jax.random.fold_in(key, 6), position), (shards_of,), jnp.float32, smallest / len(cuts), largest / len(cuts))
        return jnp.repeat(jnp.exp(draws), dims[position] // shards_of).reshape((-1,) + (1,) * (len(dims) - position - 1))

    gain = one(*cuts[0])
    for cut in cuts[1:]:
        gain = gain * one(*cut)
    return gain


def noise(rng, dims, spread, reach, pieces=(), held_as=jnp.bfloat16):
    drawn = jax.random.normal(rng, dims, jnp.float32) * spread
    if len(pieces) > 0:
        drawn = shard_levels(rng, dims, pieces, -0.22, 0.18) * drawn
    return jnp.clip(drawn, min=-reach, max=reach).astype(held_as)


def setup_inputs(seed: int = 0) -> dict:
    seeds = jax.random.split(jax.random.key(seed), 10)
    return {
        "act_in": noise(seeds[0], (SECTIONS, FRAMES, D), 1.0, 6.0, ((0, 96), (1, 8))),
        "grad_in": noise(seeds[1], (SECTIONS, FRAMES, D), 1.0, 6.0, ((0, 96), (1, 8))),
        "saved_inputs": noise(seeds[2], (SECTIONS, TICKS, FRAMES, D), 1.0, 6.0, ((0, 96), (2, 8))),
        "kernels": noise(seeds[3], (SECTIONS, RES, KW, D), KW ** -0.5, 1.0, ((0, 96),)),
        "norm_gains": jnp.clip(1.0 + 0.18 * jax.random.normal(seeds[4], (SECTIONS, RES, D), jnp.float32), 0.099609375, 1.8984375).astype(jnp.bfloat16),
        "forward_lengths": place_ends(jax.random.randint(seeds[5], (SECTIONS,), FRAMES // 2, FRAMES + 1), jax.random.fold_in(seeds[5], 1), FRAMES // 2, FRAMES).astype(jnp.int32),
        "backward_lengths": place_ends(jax.random.randint(seeds[6], (SECTIONS,), FRAMES // 2, FRAMES + 1), jax.random.fold_in(seeds[6], 1), FRAMES // 2, FRAMES).astype(jnp.int32),
        "forward_slots": place_ends(jax.random.randint(seeds[7], (SECTIONS, TICKS), 0, RES), jax.random.fold_in(seeds[7], 1), 0, RES - 1).astype(jnp.int32),
        "backward_slots": place_ends(jax.random.randint(seeds[8], (SECTIONS, TICKS), 0, RES), jax.random.fold_in(seeds[8], 1), 0, RES - 1).astype(jnp.int32),
    }


epsilon = 1e-05

def normalized(inputs):
    values = inputs.astype(jnp.float32)
    center = values - lax.optimization_barrier(jnp.mean(values, axis=-1, keepdims=True))
    inverse = lax.rsqrt(lax.optimization_barrier(jnp.mean(center * center, axis=-1, keepdims=True)) + epsilon)
    return (center * inverse, inverse)

def pick_slot(lookup, slot_id):
    onehot = (jnp.arange(lookup.shape[0], dtype=jnp.int32) == slot_id).astype(jnp.float32)
    return jnp.tensordot(onehot, lookup.astype(jnp.float32), axes=1)

def rounded(values):
    return lax.optimization_barrier(values.astype(jnp.bfloat16)).astype(jnp.float32)

def conv_taps(padded, kernel, row_count):
    total = jnp.zeros((row_count, kernel.shape[1]), jnp.float32)
    for offset in range(kernel.shape[0]):
        total = total + kernel[offset] * padded[offset:offset + row_count]
    return total

def flipped_taps(padded, kernel, row_count):
    reach_back = kernel.shape[0] - 1
    total = jnp.zeros((row_count, kernel.shape[1]), jnp.float32)
    for offset in range(kernel.shape[0]):
        total = total + kernel[offset] * padded[reach_back - offset:reach_back - offset + row_count]
    return total

def tap_products(padded, grad_mixed, row_count, tap_count):
    return jnp.stack([lax.optimization_barrier(jnp.sum(padded[offset:offset + row_count] * grad_mixed, axis=0)) for offset in range(tap_count)])

def reference(act_in, grad_in, saved_inputs, kernels, norm_gains, forward_lengths, backward_lengths, forward_slots, backward_slots):
    section_ids = jnp.arange(SECTIONS, dtype=jnp.int32)
    frame_ids = jnp.arange(FRAMES, dtype=jnp.int32)
    half_width = (KW - 1) // 2
    slot_range = jnp.arange(RES, dtype=jnp.int32)

    def prepare(inputs, kernel_set, gain_set, slot_id, length):
        kernel = pick_slot(kernel_set, slot_id)
        gain_row = pick_slot(gain_set, slot_id)
        frame_mask = (frame_ids < length).astype(jnp.float32)[:, None]
        normed, inverse = normalized(inputs)
        masked = rounded(frame_mask * gain_row * normed)
        padded = jnp.pad(masked, ((half_width, half_width), (0, 0)))
        conv_out = conv_taps(padded, kernel, FRAMES)
        return (kernel, gain_row, frame_mask, normed, inverse, padded, conv_out)

    def forward_one(packed):
        inputs, kernel_set, gain_set, slot_id, length = packed
        conv_out = prepare(inputs, kernel_set, gain_set, slot_id, length)[6]
        return (inputs.astype(jnp.float32) + conv_out * jax.nn.sigmoid(conv_out)).astype(jnp.bfloat16)

    def backward_one(packed):
        inputs, upstream, kernel_set, gain_set, slot_id, length = packed
        kernel, gain_row, frame_mask, normed, inverse, padded, conv_out = prepare(inputs, kernel_set, gain_set, slot_id, length)
        gate_back = jax.nn.sigmoid(conv_out)
        grad_up = upstream.astype(jnp.float32)
        grad_mixed = rounded(grad_up * gate_back * (1.0 + conv_out * (1.0 - gate_back)))
        tap_term = tap_products(padded, grad_mixed, FRAMES, KW)
        grad_pad = jnp.pad(grad_mixed, ((half_width, half_width), (0, 0)))
        grad_masked = frame_mask * flipped_taps(grad_pad, kernel, FRAMES)
        gain_term = lax.optimization_barrier(jnp.sum(grad_masked * normed, axis=0))
        scaled = grad_masked * gain_row
        grad_norm = inverse * (scaled - lax.optimization_barrier(jnp.mean(scaled, axis=-1, keepdims=True)) - normed * lax.optimization_barrier(jnp.mean(scaled * normed, axis=-1, keepdims=True)))
        return ((grad_up + grad_norm).astype(jnp.bfloat16), tap_term, gain_term)
    carried = act_in
    returning = grad_in
    tap_total = jnp.zeros((SECTIONS, RES, KW, D), jnp.float32)
    gain_total = jnp.zeros((SECTIONS, RES, D), jnp.float32)
    for tick_step in range(TICKS):
        ahead_len = forward_lengths[(section_ids - tick_step) % SECTIONS]
        outputs = lax.map(forward_one, (carried, kernels, norm_gains, forward_slots[:, tick_step], ahead_len))
        back_len = backward_lengths[(section_ids + tick_step) % SECTIONS]
        grad_x, tap_terms, gain_terms = lax.map(backward_one, (saved_inputs[:, tick_step], returning, kernels, norm_gains, backward_slots[:, tick_step], back_len))
        onehot = (slot_range[None, :] == backward_slots[:, tick_step][:, None]).astype(jnp.float32)
        tap_total = tap_total + onehot[:, :, None, None] * tap_terms[:, None]
        gain_total = gain_total + onehot[:, :, None] * gain_terms[:, None]
        carried = jnp.roll(outputs, 1, axis=0)
        returning = jnp.roll(grad_x, -1, axis=0)
    return (carried, returning, tap_total, gain_total)
```

```python
import functools

import jax
import jax.numpy as jnp
from jax import lax
from jax.experimental import pallas as pl
from jax.experimental.pallas import tpu as pltpu
from jax.sharding import PartitionSpec as P

epsilon = 1e-05
MESH = pl.DeviceIdType.MESH
f32 = jnp.float32
bf16 = jnp.bfloat16
LANES = 128
PAD = 16


def row(ref, use, j, c):
    return jnp.broadcast_to(ref[use, pl.ds(j, 1), pl.ds(pl.multiple_of(c * LANES, LANES), LANES)], (8, LANES))


def conv_block(m_ref, k_ref, use, c, groups, flip):
    total = [None] * groups
    for b in range(8):
        taps = {}
        for a in range(4):
            o = 8 * a + b
            if o > 0:
                taps[a] = row(k_ref, use, 31 - o if flip else o - 1, c)
        for i in range(groups + 3):
            cells = m_ref[c, pl.ds(8 * i + b, 8), :]
            for a, tap in taps.items():
                r = i - a
                if 0 <= r < groups:
                    total[r] = tap * cells if total[r] is None else total[r] + tap * cells
    return total


def tap_block(m_ref, gm_ref, tap_ref, tick, c, groups):
    grads = [gm_ref[c, pl.ds(PAD + 8 * r, 8), :] for r in range(groups)]
    lanes = pl.ds(pl.multiple_of(c * LANES, LANES), LANES)
    for b in range(8):
        total = {}
        for i in range(groups + 3):
            cells = m_ref[c, pl.ds(8 * i + b, 8), :]
            for a in range(4):
                r = i - a
                if 8 * a + b > 0 and 0 <= r < groups:
                    total[a] = grads[r] * cells + total[a] if a in total else grads[r] * cells
        for a, value in total.items():
            tap_ref[tick, pl.ds(8 * a + b - 1, 1), lanes] = jnp.sum(value, axis=0, keepdims=True)


def body(
    sections,
    shards,
    act,
    grad,
    saved,
    ksel,
    flen,
    blen,
    act_out,
    grad_out,
    fin,
    x_f,
    x_b,
    g_in,
    k_ref,
    hx,
    m_f,
    m_b,
    gm,
    dref,
    scaled,
    mean_ref,
    inv_ref,
    a_ref,
    b_ref,
    y,
    gx,
    arrive_f,
    arrive_g,
    edge_f,
    gh_send,
    gh_recv,
    tap_ref,
    rs_buf,
    red,
    local_sem,
    hx_s,
    hx_r,
    y_s,
    y_r,
    e_s,
    e_r,
    g_s,
    g_r,
    gh_s,
    gh_r,
    rs_s,
    rs_r,
    ag_s,
    ag_r,
):
    s = lax.axis_index("section")
    t = lax.axis_index("tm")
    rows, width = act.shape
    blocks = width // LANES
    groups = rows // 8
    own = width // shards
    quarter = width // 4
    quarter_blocks = blocks // 4
    after, before = lax.rem(s + 1, sections), lax.rem(s + sections - 1, sections)
    right, left = lax.rem(t + 1, shards), lax.rem(t + shards - 1, shards)
    base = t * rows

    barrier = pltpu.get_barrier_semaphore()
    peers = [(after, t), (before, t), (after, left), (after, right), (before, left), (before, right)]
    peers += [(s, lax.rem(t + d, shards)) for d in range(1, shards)]
    for peer in peers:
        pl.semaphore_signal(barrier, inc=1, device_id=peer, device_id_type=MESH)

    def local(src, dst, n):
        return pltpu.make_async_copy(src, dst, local_sem.at[n])

    loads = [
        local(act, x_f, 0),
        local(ksel, k_ref, 1),
        local(saved.at[0], x_b.at[0], 2),
        local(saved.at[1], x_b.at[1], 3),
        local(grad, g_in, 4),
    ]
    for copy in loads:
        copy.start()

    sent = []

    def remote(src, dst, send, recv, peer):
        return pltpu.make_async_remote_copy(
            src_ref=src, dst_ref=dst, send_sem=send, recv_sem=recv, device_id=peer, device_id_type=MESH
        )

    def launch(copy):
        copy.start()
        sent.append(copy)
        return copy

    def lanes_of(c):
        return pl.ds(pl.multiple_of(c * LANES, LANES), LANES)

    def normalize(load, frame, length, use, m_ref, at, keep=None):
        cells = [load(c) for c in range(blocks)]
        total = cells[0]
        for c in range(1, blocks):
            total = total + cells[c]
        mean = jnp.sum(total, axis=1, keepdims=True) * (1.0 / width)
        cells = [v - mean for v in cells]
        total = cells[0] * cells[0]
        for c in range(1, blocks):
            total = total + cells[c] * cells[c]
        var = jnp.sum(total, axis=1, keepdims=True) * (1.0 / width)
        inverse = lax.rsqrt(var + epsilon)
        ids = frame + lax.broadcasted_iota(jnp.int32, (16, LANES), 0)
        mask = jnp.where((ids >= 0) & (ids < length), 1.0, 0.0).astype(f32)
        scale = mask * inverse
        for c in range(blocks):
            gain = row(k_ref, use, 31, c)
            m_ref[c, pl.ds(at, 16), :] = cells[c] * scale * jnp.concatenate([gain, gain], axis=0)
        if keep is not None:
            mean_ref[keep, pl.ds(at - PAD, 16), :] = jnp.broadcast_to(mean, (16, LANES))
            inv_ref[keep, pl.ds(at - PAD, 16), :] = jnp.broadcast_to(inverse, (16, LANES))

    def norm_own(x_ref, length, use, m_ref, keep=None):
        @pl.loop(0, rows // 16)
        def _(i):
            r = pl.multiple_of(i * 16, 16)
            normalize(
                lambda c: x_ref[pl.ds(r, 16), pl.ds(c * LANES, LANES)].astype(f32),
                base + r,
                length,
                use,
                m_ref,
                pl.multiple_of(PAD + r, 16),
                keep,
            )

    def norm_edges(h_ref, length, use, m_ref):
        @pl.loop(0, 2)
        def _(side):
            normalize(
                lambda c: h_ref[side, :, pl.ds(c * LANES, LANES)].astype(f32),
                base - PAD + side * (rows + PAD),
                length,
                use,
                m_ref,
                pl.multiple_of(side * (rows + PAD), 16),
            )

    f_len = [flen[lax.rem(s + sections - k, sections)] for k in range(2)]
    b_len = [blen[lax.rem(s + k, sections)] for k in range(2)]

    loads[0].wait()
    loads[1].wait()
    norm_own(x_f, f_len[0], 0, m_f)
    pl.semaphore_wait(barrier, len(peers))

    halos = []
    for n, ref in ((0, act), (1, saved.at[0]), (2, saved.at[1])):
        pair = []
        for side, peer in ((1, left), (0, right)):
            edge = pl.ds(0, 16) if side == 1 else pl.ds(rows - 16, 16)
            pair.append(launch(remote(ref.at[edge], hx.at[n, side], hx_s.at[n, side], hx_r.at[n, side], (s, peer))))
        halos.append(pair)

    loads[2].wait()
    norm_own(x_b.at[0], b_len[0], 2, m_b.at[0], 0)
    loads[3].wait()
    norm_own(x_b.at[1], b_len[1], 3, m_b.at[1], 1)

    def forward(tick, x_ref, dst):
        copies = [
            remote(
                y.at[tick, :, pl.ds(q * quarter, quarter)],
                dst.at[:, pl.ds(q * quarter, quarter)],
                y_s.at[tick, q],
                y_r.at[tick, q],
                (after, t),
            )
            for q in range(4)
        ]

        @pl.loop(0, blocks)
        def _(c):
            total = conv_block(m_f, k_ref, tick, c, groups, False)
            for r in range(groups // 2):
                conv = jnp.concatenate(total[2 * r : 2 * r + 2], axis=0)
                x = x_ref[pl.ds(16 * r, 16), lanes_of(c)].astype(f32)
                y[tick, pl.ds(16 * r, 16), lanes_of(c)] = (x + conv * jax.nn.sigmoid(conv)).astype(bf16)
            for q in range(4):

                @pl.when(c == (q + 1) * quarter_blocks - 1)
                def _():
                    copies[q].start()

        sent.extend(copies)
        return copies

    def slope(conv):
        gate = jax.nn.sigmoid(conv)
        return gate * (1.0 + conv * (1.0 - gate))

    def put_mixed(tick, c, r, value):
        gm[c, pl.ds(PAD + 16 * r, 16), :] = value
        if r == 0:
            gh_send[tick, 1, :, lanes_of(c)] = value.astype(bf16)
        if r == groups // 2 - 1:
            gh_send[tick, 0, :, lanes_of(c)] = value.astype(bf16)

    def send_mixed(tick):
        return [
            launch(
                remote(
                    gh_send.at[tick, side],
                    gh_recv.at[tick, side],
                    gh_s.at[tick, side],
                    gh_r.at[tick, side],
                    (s, peer),
                )
            )
            for side, peer in ((1, left), (0, right))
        ]

    def taps(tick):
        @pl.loop(0, blocks)
        def _(c):
            tap_block(m_b.at[tick], gm, tap_ref, tick, c, groups)

    def mixed_edges(tick, copies):
        for copy in copies:
            copy.wait_recv()
        inside = (jnp.where(t > 0, 1.0, 0.0), jnp.where(t < shards - 1, 1.0, 0.0))

        @pl.loop(0, blocks)
        def _(c):
            for side in range(2):
                gm[c, pl.ds(side * (rows + PAD), 16), :] = gh_recv[tick, side, :, lanes_of(c)].astype(f32) * inside[side]

    def normed(tick, r, c):
        x = x_b[tick, pl.ds(r, 16), lanes_of(c)].astype(f32)
        return (x - mean_ref[tick, pl.ds(r, 16), :]) * inv_ref[tick, pl.ds(r, 16), :]

    def input_grad(tick, g_ref, dst):
        use = 2 + tick
        a_ref[...] = jnp.zeros_like(a_ref)
        b_ref[...] = jnp.zeros_like(b_ref)

        @pl.loop(0, blocks)
        def _(c):
            total = conv_block(gm, k_ref, use, c, groups, True)
            gain = row(k_ref, use, 31, c)
            gain = jnp.concatenate([gain, gain], axis=0)
            ids = base + lax.broadcasted_iota(jnp.int32, (16, LANES), 0)
            term = None
            for r in range(groups // 2):
                value = jnp.concatenate(total[2 * r : 2 * r + 2], axis=0)
                value = jnp.where(ids < b_len[tick] - 16 * r, value, 0.0)
                norm = normed(tick, 16 * r, c)
                part = value * norm
                term = part if term is None else term + part
                value = value * gain
                at = pl.ds(16 * r, 16)
                scaled[c, at, :] = value
                a_ref[at, :] += value
                b_ref[at, :] += value * norm
            tap_ref[tick, pl.ds(31, 1), lanes_of(c)] = jnp.sum(term, axis=0, keepdims=True)

        copies = [
            remote(
                gx.at[tick, pl.ds(q * (rows // 4), rows // 4)],
                dst.at[pl.ds(q * (rows // 4), rows // 4)],
                g_s.at[tick, q],
                g_r.at[tick, q],
                (before, t),
            )
            for q in range(4)
        ]

        @pl.loop(0, rows // 16)
        def _(i):
            r = pl.multiple_of(i * 16, 16)
            at = pl.ds(r, 16)
            mean_a = jnp.sum(a_ref[at, :], axis=1, keepdims=True) * (1.0 / width)
            mean_b = jnp.sum(b_ref[at, :], axis=1, keepdims=True) * (1.0 / width)
            inverse = inv_ref[tick, at, :]
            for c in range(blocks):
                lanes = pl.ds(c * LANES, LANES)
                norm = (x_b[tick, at, lanes].astype(f32) - mean_ref[tick, at, :]) * inverse
                value = (scaled[c, at, :] - mean_a - norm * mean_b) * inverse
                gx[tick, at, lanes] = (g_ref[at, lanes].astype(f32) + value).astype(bf16)
            for q in range(4):

                @pl.when(i == (q + 1) * (rows // 64) - 1)
                def _():
                    copies[q].start()

        sent.extend(copies)
        return copies

    def scatter(tick):
        for d in range(1, shards):
            peer = lax.rem(t + d, shards)
            lanes = pl.ds(pl.multiple_of(peer * own, LANES), own)
            launch(
                remote(
                    tap_ref.at[tick, :, lanes],
                    rs_buf.at[tick, t],
                    rs_s.at[tick, d],
                    rs_r.at[tick, t],
                    (s, peer),
                )
            )

    def gather(tick):
        mine = pl.ds(pl.multiple_of(t * own, LANES), own)
        for d in range(1, shards):
            peer = lax.rem(t + d, shards)
            remote(
                tap_ref.at[tick, :, mine], rs_buf.at[tick, peer], rs_s.at[tick, d], rs_r.at[tick, peer], (s, peer)
            ).wait_recv()
        value = tap_ref[tick, :, mine]
        for d in range(1, shards):
            value = value + rs_buf[tick, lax.rem(t + d, shards)]
        red[tick] = value
        keep = local(red.at[tick], fin.at[tick, :, mine], 5 + tick)
        keep.start()
        loads.append(keep)
        for d in range(1, shards):
            launch(
                remote(
                    red.at[tick],
                    fin.at[tick, :, mine],
                    ag_s.at[tick, d],
                    ag_r.at[tick, t],
                    (s, lax.rem(t + d, shards)),
                )
            )

    def gathered(tick):
        for d in range(1, shards):
            peer = lax.rem(t + d, shards)
            theirs = pl.ds(pl.multiple_of(peer * own, LANES), own)
            remote(red.at[tick], fin.at[tick, :, theirs], ag_s.at[tick, d], ag_r.at[tick, peer], (s, peer)).wait_recv()

    for copy in halos[0]:
        copy.wait_recv()
    norm_edges(hx.at[0], f_len[0], 0, m_f)
    ahead = forward(0, x_f, arrive_f)
    edges = []
    for side, peer in ((1, left), (0, right)):
        edge = pl.ds(0, 16) if side == 1 else pl.ds(rows - 16, 16)
        edges.append(launch(remote(y.at[0, edge], edge_f.at[side], e_s.at[side], e_r.at[side], (after, peer))))

    for copy in halos[1]:
        copy.wait_recv()
    norm_edges(hx.at[1], b_len[0], 2, m_b.at[0])
    loads[4].wait()

    @pl.loop(0, blocks)
    def _(c):
        total = conv_block(m_b.at[0], k_ref, 2, c, groups, False)
        for r in range(groups // 2):
            conv = jnp.concatenate(total[2 * r : 2 * r + 2], axis=0)
            put_mixed(0, c, r, g_in[pl.ds(16 * r, 16), lanes_of(c)].astype(f32) * slope(conv))

    mixed = send_mixed(0)
    taps(0)
    mixed_edges(0, mixed)
    behind = input_grad(0, g_in, arrive_g)
    scatter(0)

    for copy in halos[2]:
        copy.wait_recv()
    norm_edges(hx.at[2], b_len[1], 3, m_b.at[1])

    @pl.loop(0, blocks)
    def _(c):
        total = conv_block(m_b.at[1], k_ref, 3, c, groups, False)
        for r in range(groups // 2):
            conv = jnp.concatenate(total[2 * r : 2 * r + 2], axis=0)
            dref[c, pl.ds(16 * r, 16), :] = slope(conv)

    gather(0)

    for copy in ahead + edges:
        copy.wait_recv()
    norm_own(arrive_f, f_len[1], 1, m_f)
    norm_edges(edge_f, f_len[1], 1, m_f)
    ahead = forward(1, arrive_f, act_out)

    for copy in behind:
        copy.wait_recv()

    @pl.loop(0, blocks)
    def _(c):
        for r in range(groups // 2):
            at = pl.ds(16 * r, 16)
            put_mixed(1, c, r, arrive_g[at, lanes_of(c)].astype(f32) * dref[c, at, :])

    mixed = send_mixed(1)
    taps(1)
    mixed_edges(1, mixed)
    behind = input_grad(1, arrive_g, grad_out)
    scatter(1)
    gather(1)
    gathered(0)
    gathered(1)
    for copy in ahead + behind:
        copy.wait_recv()
    for copy in sent:
        copy.wait_send()
    for copy in loads[5:]:
        copy.wait()


def relay(sections, shards, act, grad, saved, ksel, flen, blen):
    rows, width = act.shape
    blocks = width // LANES
    own = width // shards
    vm = pltpu.VMEM
    dma = pltpu.SemaphoreType.DMA
    padded_rows = rows + 2 * PAD
    anywhere = pl.BlockSpec(memory_space=pl.ANY)
    scalars = pl.BlockSpec(memory_space=pltpu.SMEM)
    return pl.pallas_call(
        functools.partial(body, sections, shards),
        out_shape=[
            jax.ShapeDtypeStruct((rows, width), bf16),
            jax.ShapeDtypeStruct((rows, width), bf16),
            jax.ShapeDtypeStruct((2, 32, width), f32),
        ],
        in_specs=[anywhere] * 4 + [scalars] * 2,
        out_specs=[anywhere] * 3,
        scratch_shapes=[
            vm((rows, width), bf16),
            vm((2, rows, width), bf16),
            vm((rows, width), bf16),
            vm((4, 32, width), f32),
            vm((3, 2, 16, width), bf16),
            vm((blocks, padded_rows, LANES), f32),
            vm((2, blocks, padded_rows, LANES), f32),
            vm((blocks, padded_rows, LANES), f32),
            vm((blocks, rows, LANES), f32),
            vm((blocks, rows, LANES), f32),
            vm((2, rows, LANES), f32),
            vm((2, rows, LANES), f32),
            vm((rows, LANES), f32),
            vm((rows, LANES), f32),
            vm((2, rows, width), bf16),
            vm((2, rows, width), bf16),
            vm((rows, width), bf16),
            vm((rows, width), bf16),
            vm((2, 16, width), bf16),
            vm((2, 2, 16, width), bf16),
            vm((2, 2, 16, width), bf16),
            vm((2, 32, width), f32),
            vm((2, shards, 32, own), f32),
            vm((2, 32, own), f32),
            dma((7,)),
            dma((3, 2)),
            dma((3, 2)),
            dma((2, 4)),
            dma((2, 4)),
            dma((2,)),
            dma((2,)),
            dma((2, 4)),
            dma((2, 4)),
            dma((2, 2)),
            dma((2, 2)),
            dma((2, shards)),
            dma((2, shards)),
            dma((2, shards)),
            dma((2, shards)),
        ],
        compiler_params=pltpu.CompilerParams(collective_id=0, has_side_effects=True, vmem_limit_bytes=56 << 20),
        name="relay",
    )(act, grad, saved, ksel, flen, blen)


def local_step(
    act_in,
    grad_in,
    saved_inputs,
    kernels,
    norm_gains,
    forward_lengths,
    backward_lengths,
    forward_slots,
    backward_slots,
):
    sections = lax.axis_size("section")
    shards = lax.axis_size("tm")
    s = lax.axis_index("section")
    stack = jnp.concatenate([kernels[0], norm_gains[0][:, None, :]], axis=1)
    back = backward_slots[s]
    slots = jnp.concatenate([forward_slots[s], back])
    ksel = jnp.where(slots[:, None, None] == 0, stack[0][None], stack[1][None]).astype(f32)
    act_out, grad_out, fin = relay(
        sections, shards, act_in[0], grad_in[0], saved_inputs[0], ksel, forward_lengths, backward_lengths
    )
    onehot = (jnp.arange(kernels.shape[1], dtype=jnp.int32)[:, None] == back[None, :]).astype(f32)
    total = onehot[:, 0, None, None] * fin[0][None] + onehot[:, 1, None, None] * fin[1][None]
    return (act_out[None], grad_out[None], total[None, :, :31], total[None, :, 31])


def solution(mesh):
    in_specs = (
        P("section", "tm", None),
        P("section", "tm", None),
        P("section", None, "tm", None),
        P("section", None, None, None),
        P("section", None, None),
        P(),
        P(),
        P(),
        P(),
    )
    out_specs = (
        P("section", "tm", None),
        P("section", "tm", None),
        P("section", None, None, None),
        P("section", None, None),
    )
    return jax.shard_map(local_step, mesh=mesh, in_specs=in_specs, out_specs=out_specs, check_vma=False)
```

```python
import functools

import jax
import jax.numpy as jnp
from jax import lax
from jax.experimental import pallas as pl
from jax.experimental.pallas import tpu as pltpu
from jax.sharding import PartitionSpec as P

epsilon = 1e-05
MESH = pl.DeviceIdType.MESH
f32 = jnp.float32
bf16 = jnp.bfloat16
LANES = 128
PAD = 16


def row(ref, use, j, c):
    return jnp.broadcast_to(ref[use, pl.ds(j, 1), pl.ds(pl.multiple_of(c * LANES, LANES), LANES)], (8, LANES))


def conv_block(m_ref, k_ref, use, c, first, groups, flip):
    total = [None] * groups
    for b in range(8):
        taps = {}
        for a in range(4):
            o = 8 * a + b
            if o > 0:
                taps[a] = row(k_ref, use, 31 - o if flip else o - 1, c)
        for i in range(groups + 3):
            cells = m_ref[c, pl.ds(8 * (first + i) + b, 8), :]
            for a, tap in taps.items():
                r = i - a
                if 0 <= r < groups:
                    total[r] = tap * cells if total[r] is None else total[r] + tap * cells
    return total


def tap_block(m_ref, gm_ref, tap_ref, tick, c, groups):
    grads = [gm_ref[c, pl.ds(PAD + 8 * r, 8), :] for r in range(groups)]
    lanes = pl.ds(pl.multiple_of(c * LANES, LANES), LANES)
    for b in range(8):
        total = {}
        for i in range(groups + 3):
            cells = m_ref[c, pl.ds(8 * i + b, 8), :]
            for a in range(4):
                r = i - a
                if 8 * a + b > 0 and 0 <= r < groups:
                    total[a] = grads[r] * cells + total[a] if a in total else grads[r] * cells
        for a, value in total.items():
            tap_ref[tick, pl.ds(8 * a + b - 1, 1), lanes] = jnp.sum(value, axis=0, keepdims=True)


def body(
    sections,
    shards,
    act,
    grad,
    saved,
    kernels,
    gains,
    flen,
    blen,
    fslot,
    bslot,
    act_out,
    grad_out,
    fin,
    x_f,
    x_b,
    g_in,
    k_raw,
    gain_raw,
    k_ref,
    hx,
    m_f,
    m_b,
    gm,
    dref,
    scaled,
    mean_ref,
    inv_ref,
    a_ref,
    b_ref,
    y,
    gx,
    arrive_f,
    arrive_g,
    edge_f,
    gh_send,
    gh_recv,
    tap_ref,
    tap_bf,
    rs_buf,
    part,
    part_in,
    red,
    local_sem,
    hx_s,
    hx_r,
    y_s,
    y_r,
    e_s,
    e_r,
    g_s,
    g_r,
    gh_s,
    gh_r,
    rs_s,
    rs_r,
    pr_s,
    pr_r,
    ag_s,
    ag_r,
):
    s = lax.axis_index("section")
    t = lax.axis_index("tm")
    rows, width = act.shape
    blocks = width // LANES
    tiles = rows // 16
    quarter = width // 4
    quarter_blocks = blocks // 4
    band = rows // 4
    line = shards // 2
    own = width // line
    t_x, t_y = lax.rem(t, line), lax.div(t, line)
    after, before = lax.rem(s + 1, sections), lax.rem(s + sections - 1, sections)
    right, left = lax.rem(t + 1, shards), lax.rem(t + shards - 1, shards)
    base = t * rows
    outer = ((0, band // 8), (3 * band // 8, band // 8))
    inner = ((band // 8, band // 4),)

    barrier = pltpu.get_barrier_semaphore()
    peers = [(after, t), (before, t), (after, left), (after, right), (before, left), (before, right)]
    peers += [(s, lax.rem(t + d, shards)) for d in range(1, shards)]
    for peer in peers:
        pl.semaphore_signal(barrier, inc=1, device_id=peer, device_id_type=MESH)

    def local(src, dst, n):
        return pltpu.make_async_copy(src, dst, local_sem.at[n])

    loads = [
        local(kernels, k_raw, 0),
        local(gains, gain_raw, 1),
        local(saved.at[0], x_b.at[0], 2),
        local(act, x_f, 3),
        local(saved.at[1], x_b.at[1], 4),
        local(grad, g_in, 5),
    ]
    for copy in loads:
        copy.start()

    sent = []

    def remote(src, dst, send, recv, peer):
        return pltpu.make_async_remote_copy(
            src_ref=src, dst_ref=dst, send_sem=send, recv_sem=recv, device_id=peer, device_id_type=MESH
        )

    def launch(copy):
        copy.start()
        sent.append(copy)
        return copy

    def lanes_of(c):
        return pl.ds(pl.multiple_of(c * LANES, LANES), LANES)

    def twice(value):
        return jnp.concatenate([value, value], axis=0)

    f_len = [flen[lax.rem(s + sections - k, sections)] for k in range(2)]
    b_len = [blen[lax.rem(s + k, sections)] for k in range(2)]
    slots = [fslot[0, s], fslot[1, s], bslot[0, s], bslot[1, s]]

    def pick(use):
        one = slots[use].astype(f32)
        zero = 1.0 - one
        pair = gain_raw[...].astype(f32)
        k_ref[use, pl.ds(31, 1), :] = pair[0:1] * zero + pair[1:2] * one

        for j in range(31):
            pair = k_raw[j].astype(f32)
            k_ref[use, pl.ds(j, 1), :] = pair[0:1] * zero + pair[1:2] * one

    def normalize(load, count, frames, at, length, use, m_ref, keep=None):
        zeros = [jnp.zeros((16, LANES), f32)] * count

        def sums(c, totals):
            return [total + load(n, c) for n, total in enumerate(totals)]

        totals = lax.fori_loop(0, blocks, sums, zeros, unroll=4)
        means = [
            jnp.broadcast_to(jnp.sum(total, axis=1, keepdims=True) * (1.0 / width), (16, LANES)) for total in totals
        ]

        def squares(c, totals):
            out = []
            for n, total in enumerate(totals):
                center = load(n, c) - means[n]
                out.append(total + center * center)
            return out

        totals = lax.fori_loop(0, blocks, squares, zeros, unroll=4)
        scales = []
        for n, total in enumerate(totals):
            var = jnp.sum(total, axis=1, keepdims=True) * (1.0 / width)
            inverse = jnp.broadcast_to(lax.rsqrt(var + epsilon), (16, LANES))
            if keep is not None:
                mean_ref[keep, pl.ds(16 * n, 16), :] = means[n]
                inv_ref[keep, pl.ds(16 * n, 16), :] = inverse
            ids = frames[n] + lax.broadcasted_iota(jnp.int32, (16, LANES), 0)
            scales.append(jnp.where((ids >= 0) & (ids < length), inverse, 0.0))

        def write(c, _):
            gain = twice(row(k_ref, use, 31, c))
            for n in range(count):
                m_ref[c, pl.ds(at[n], 16), :] = (load(n, c) - means[n]) * scales[n] * gain
            return 0

        lax.fori_loop(0, blocks, write, 0, unroll=2)

    def norm_own(x_ref, length, use, m_ref, keep=None):
        normalize(
            lambda n, c: x_ref[pl.ds(16 * n, 16), lanes_of(c)].astype(f32),
            tiles,
            [base + 16 * n for n in range(tiles)],
            [PAD + 16 * n for n in range(tiles)],
            length,
            use,
            m_ref,
            keep,
        )

    def norm_edges(h_ref, length, use, m_ref):
        normalize(
            lambda n, c: h_ref[n, :, lanes_of(c)].astype(f32),
            2,
            [base - PAD, base + rows],
            [0, rows + PAD],
            length,
            use,
            m_ref,
        )

    loads[0].wait()
    loads[1].wait()
    pick(2)
    pl.semaphore_wait(barrier, len(peers))

    halos = {}
    for n, ref in ((1, saved.at[0]), (0, act), (2, saved.at[1])):
        halos[n] = []
        for side, peer in ((1, left), (0, right)):
            edge = pl.ds(0, 16) if side == 1 else pl.ds(rows - 16, 16)
            halos[n].append(
                launch(remote(ref.at[edge], hx.at[n, side], hx_s.at[n, side], hx_r.at[n, side], (s, peer)))
            )

    loads[2].wait()
    norm_own(x_b.at[0], b_len[0], 2, m_b.at[0], 0)
    loads[3].wait()
    pick(0)
    norm_own(x_f, f_len[0], 0, m_f)

    def forward(tick, x_ref, dst):
        copies = [
            remote(
                y.at[tick, :, pl.ds(q * quarter, quarter)],
                dst.at[:, pl.ds(q * quarter, quarter)],
                y_s.at[tick, q],
                y_r.at[tick, q],
                (after, t),
            )
            for q in range(4)
        ]

        @pl.loop(0, blocks)
        def _(c):
            total = conv_block(m_f, k_ref, tick, c, 0, 2 * tiles, False)
            for r in range(tiles):
                conv = jnp.concatenate(total[2 * r : 2 * r + 2], axis=0)
                x = x_ref[pl.ds(16 * r, 16), lanes_of(c)].astype(f32)
                y[tick, pl.ds(16 * r, 16), lanes_of(c)] = (x + conv * jax.nn.sigmoid(conv)).astype(bf16)
            for q in range(4):

                @pl.when(c == (q + 1) * quarter_blocks - 1)
                def _():
                    copies[q].start()

        sent.extend(copies)
        return copies

    def slope(conv):
        gate = jax.nn.sigmoid(conv)
        return gate * (1.0 + conv * (1.0 - gate))

    def put_mixed(tick, c, r, value):
        gm[c, pl.ds(PAD + 16 * r, 16), :] = value
        if r == 0:
            gh_send[tick, 1, :, lanes_of(c)] = value.astype(bf16)
        if r == tiles - 1:
            gh_send[tick, 0, :, lanes_of(c)] = value.astype(bf16)

    def send_mixed(tick):
        return [
            launch(
                remote(
                    gh_send.at[tick, side],
                    gh_recv.at[tick, side],
                    gh_s.at[tick, side],
                    gh_r.at[tick, side],
                    (s, peer),
                )
            )
            for side, peer in ((1, left), (0, right))
        ]

    def taps(tick):
        @pl.loop(0, blocks)
        def _(c):
            tap_block(m_b.at[tick], gm, tap_ref, tick, c, 2 * tiles)

        tap_bf[tick] = tap_ref[tick].astype(bf16)

    def mixed_edges(tick, copies):
        for copy in copies:
            copy.wait_recv()
        inside = (jnp.where(t > 0, 1.0, 0.0), jnp.where(t < shards - 1, 1.0, 0.0))

        @pl.loop(0, blocks)
        def _(c):
            for side in range(2):
                gm[c, pl.ds(side * (rows + PAD), 16), :] = gh_recv[tick, side, :, lanes_of(c)].astype(f32) * inside[side]

    def normed(tick, r, c):
        x = x_b[tick, pl.ds(r, 16), lanes_of(c)].astype(f32)
        return (x - mean_ref[tick, pl.ds(r, 16), :]) * inv_ref[tick, pl.ds(r, 16), :]

    def input_grad(tick, g_ref, dst):
        use = 2 + tick
        a_ref[...] = jnp.zeros_like(a_ref)
        b_ref[...] = jnp.zeros_like(b_ref)
        copies = {}
        for turn, (segments, bands) in enumerate(((outer, (0, 3)), (inner, (1, 2)))):

            @pl.loop(0, blocks)
            def _(c):
                gain = twice(row(k_ref, use, 31, c))
                ids = base + lax.broadcasted_iota(jnp.int32, (16, LANES), 0)
                term = None
                for first, groups in segments:
                    total = conv_block(gm, k_ref, use, c, first, groups, True)
                    for n in range(groups // 2):
                        r = 8 * first + 16 * n
                        value = jnp.concatenate(total[2 * n : 2 * n + 2], axis=0)
                        value = jnp.where(ids < b_len[tick] - r, value, 0.0)
                        norm = normed(tick, r, c)
                        part_term = value * norm
                        term = part_term if term is None else term + part_term
                        value = value * gain
                        at = pl.ds(r, 16)
                        scaled[c, at, :] = value
                        a_ref[at, :] += value
                        b_ref[at, :] += value * norm
                total_term = jnp.sum(term, axis=0, keepdims=True)
                if turn > 0:
                    total_term = total_term + tap_ref[tick, pl.ds(31, 1), lanes_of(c)]
                tap_ref[tick, pl.ds(31, 1), lanes_of(c)] = total_term

            starts = [q * band + 16 * n for q in bands for n in range(band // 16)]
            fixed = []
            for r in starts:
                at = pl.ds(r, 16)
                mean_a = jnp.broadcast_to(jnp.sum(a_ref[at, :], axis=1, keepdims=True) * (1.0 / width), (16, LANES))
                mean_b = jnp.broadcast_to(jnp.sum(b_ref[at, :], axis=1, keepdims=True) * (1.0 / width), (16, LANES))
                fixed.append((mean_a, mean_b))
            for (mean_a, mean_b), r in zip(fixed, starts):
                a_ref[pl.ds(r, 16), :] = mean_a
                b_ref[pl.ds(r, 16), :] = mean_b
            for q in bands:
                mine = [q * band + 16 * n for n in range(band // 16)]
                held = [
                    [ref[pl.ds(r, 16), :] for ref in (a_ref, b_ref, mean_ref.at[tick], inv_ref.at[tick])] for r in mine
                ]

                def write(c, _):
                    for r, (mean_a, mean_b, mean, inverse) in zip(mine, held):
                        at = pl.ds(r, 16)
                        norm = (x_b[tick, at, lanes_of(c)].astype(f32) - mean) * inverse
                        value = (scaled[c, at, :] - mean_a - norm * mean_b) * inverse
                        gx[tick, at, lanes_of(c)] = (g_ref[at, lanes_of(c)].astype(f32) + value).astype(bf16)
                    return 0

                lax.fori_loop(0, blocks, write, 0, unroll=2)
                copies[q] = launch(
                    remote(
                        gx.at[tick, pl.ds(q * band, band)],
                        dst.at[pl.ds(q * band, band)],
                        g_s.at[tick, q],
                        g_r.at[tick, q],
                        (before, t),
                    )
                )
        return copies

    def lane_part(n):
        return pl.ds(pl.multiple_of(n * own, LANES), own)

    def scatter(tick):
        for d in range(1, line):
            peer = lax.rem(t_x + d, line)
            launch(
                remote(
                    tap_bf.at[tick, :, lane_part(peer)],
                    rs_buf.at[tick, t_x],
                    rs_s.at[tick, d],
                    rs_r.at[tick, t_x],
                    (s, t_y * line + peer),
                )
            )

    def exchange(tick):
        value = tap_ref[tick, :, lane_part(t_x)]
        for d in range(1, line):
            peer = lax.rem(t_x + d, line)
            remote(
                tap_bf.at[tick, :, lane_part(peer)],
                rs_buf.at[tick, peer],
                rs_s.at[tick, d],
                rs_r.at[tick, peer],
                (s, t_y * line + peer),
            ).wait_recv()
            value = value + rs_buf[tick, peer].astype(f32)
        part[tick] = value.astype(bf16)
        return launch(
            remote(part.at[tick], part_in.at[tick], pr_s.at[tick], pr_r.at[tick], (s, (1 - t_y) * line + t_x))
        )

    def gather(tick, swap):
        swap.wait_recv()
        red[tick] = (part[tick].astype(f32) + part_in[tick].astype(f32)).astype(bf16)
        keep = local(red.at[tick], fin.at[tick, :, lane_part(t_x)], 6 + tick)
        keep.start()
        loads.append(keep)
        for d in range(1, line):
            launch(
                remote(
                    red.at[tick],
                    fin.at[tick, :, lane_part(t_x)],
                    ag_s.at[tick, d],
                    ag_r.at[tick, t_x],
                    (s, t_y * line + lax.rem(t_x + d, line)),
                )
            )

    def gathered(tick):
        for d in range(1, line):
            peer = lax.rem(t_x + d, line)
            remote(
                red.at[tick],
                fin.at[tick, :, lane_part(peer)],
                ag_s.at[tick, d],
                ag_r.at[tick, peer],
                (s, t_y * line + peer),
            ).wait_recv()

    for copy in halos[1]:
        copy.wait_recv()
    norm_edges(hx.at[1], b_len[0], 2, m_b.at[0])
    loads[5].wait()

    @pl.loop(0, blocks)
    def _(c):
        total = conv_block(m_b.at[0], k_ref, 2, c, 0, 2 * tiles, False)
        for r in range(tiles):
            conv = jnp.concatenate(total[2 * r : 2 * r + 2], axis=0)
            put_mixed(0, c, r, g_in[pl.ds(16 * r, 16), lanes_of(c)].astype(f32) * slope(conv))

    mixed = send_mixed(0)
    for copy in halos[0]:
        copy.wait_recv()
    norm_edges(hx.at[0], f_len[0], 0, m_f)
    ahead = forward(0, x_f, arrive_f)
    edges = []
    for side, peer in ((1, left), (0, right)):
        edge = pl.ds(0, 16) if side == 1 else pl.ds(rows - 16, 16)
        edges.append(launch(remote(y.at[0, edge], edge_f.at[side], e_s.at[side], e_r.at[side], (after, peer))))
    mixed_edges(0, mixed)
    behind = input_grad(0, g_in, arrive_g)
    taps(0)
    scatter(0)

    loads[4].wait()
    pick(3)
    norm_own(x_b.at[1], b_len[1], 3, m_b.at[1], 1)
    for copy in halos[2]:
        copy.wait_recv()
    norm_edges(hx.at[2], b_len[1], 3, m_b.at[1])

    @pl.loop(0, blocks)
    def _(c):
        total = conv_block(m_b.at[1], k_ref, 3, c, 0, 2 * tiles, False)
        for r in range(tiles):
            conv = jnp.concatenate(total[2 * r : 2 * r + 2], axis=0)
            dref[c, pl.ds(16 * r, 16), :] = slope(conv)

    pick(1)
    swap = exchange(0)

    def mix_bands(bands):
        for q in bands:
            behind[q].wait_recv()

        @pl.loop(0, blocks)
        def _(c):
            for q in bands:
                for r in range(q * band // 16, (q + 1) * band // 16):
                    at = pl.ds(16 * r, 16)
                    put_mixed(1, c, r, arrive_g[at, lanes_of(c)].astype(f32) * dref[c, at, :])

    mix_bands((0, 3))
    mixed = send_mixed(1)
    gather(0, swap)
    for copy in ahead + edges:
        copy.wait_recv()
    norm_own(arrive_f, f_len[1], 1, m_f)
    norm_edges(edge_f, f_len[1], 1, m_f)
    ahead = forward(1, arrive_f, act_out)
    mix_bands((1, 2))
    mixed_edges(1, mixed)
    behind = input_grad(1, arrive_g, grad_out)
    taps(1)
    scatter(1)
    swap = exchange(1)
    gather(1, swap)
    gathered(0)
    gathered(1)
    for copy in ahead + list(behind.values()):
        copy.wait_recv()
    for copy in sent:
        copy.wait_send()
    for copy in loads[6:]:
        copy.wait()


def relay(sections, shards, act, grad, saved, kernels, gains, flen, blen, fslot, bslot):
    rows, width = act.shape
    blocks = width // LANES
    line = shards // 2
    own = width // line
    vm = pltpu.VMEM
    dma = pltpu.SemaphoreType.DMA
    padded_rows = rows + 2 * PAD
    anywhere = pl.BlockSpec(memory_space=pl.ANY)
    scalars = pl.BlockSpec(memory_space=pltpu.SMEM)
    return pl.pallas_call(
        functools.partial(body, sections, shards),
        out_shape=[
            jax.ShapeDtypeStruct((rows, width), bf16),
            jax.ShapeDtypeStruct((rows, width), bf16),
            jax.ShapeDtypeStruct((2, 32, width), bf16),
        ],
        in_specs=[anywhere] * 5 + [scalars] * 4,
        out_specs=[anywhere] * 3,
        scratch_shapes=[
            vm((rows, width), bf16),
            vm((2, rows, width), bf16),
            vm((rows, width), bf16),
            vm((31, 2, width), bf16),
            vm((2, width), bf16),
            vm((4, 32, width), f32),
            vm((3, 2, 16, width), bf16),
            vm((blocks, padded_rows, LANES), f32),
            vm((2, blocks, padded_rows, LANES), f32),
            vm((blocks, padded_rows, LANES), f32),
            vm((blocks, rows, LANES), f32),
            vm((blocks, rows, LANES), f32),
            vm((2, rows, LANES), f32),
            vm((2, rows, LANES), f32),
            vm((rows, LANES), f32),
            vm((rows, LANES), f32),
            vm((2, rows, width), bf16),
            vm((2, rows, width), bf16),
            vm((rows, width), bf16),
            vm((rows, width), bf16),
            vm((2, 16, width), bf16),
            vm((2, 2, 16, width), bf16),
            vm((2, 2, 16, width), bf16),
            vm((2, 32, width), f32),
            vm((2, 32, width), bf16),
            vm((2, line, 32, own), bf16),
            vm((2, 32, own), bf16),
            vm((2, 32, own), bf16),
            vm((2, 32, own), bf16),
            dma((8,)),
            dma((3, 2)),
            dma((3, 2)),
            dma((2, 4)),
            dma((2, 4)),
            dma((2,)),
            dma((2,)),
            dma((2, 4)),
            dma((2, 4)),
            dma((2, 2)),
            dma((2, 2)),
            dma((2, line)),
            dma((2, line)),
            dma((2,)),
            dma((2,)),
            dma((2, line)),
            dma((2, line)),
        ],
        compiler_params=pltpu.CompilerParams(collective_id=0, has_side_effects=True, vmem_limit_bytes=56 << 20),
        name="relay",
    )(act, grad, saved, kernels, gains, flen, blen, fslot, bslot)


def finish_body(section, bslot, act, grad, fin, act_out, grad_out, tap_out, gain_out, wide, fin_v, full, taps, gains, sem_in, sem_out):
    rows = act.shape[0]
    half = rows // 2
    moves = []
    for n, (src, dst) in enumerate(((act, act_out), (grad, grad_out))):
        for h in range(2):
            at = pl.ds(h * half, half)
            k = 2 * n + h
            moves.append(
                (
                    pltpu.make_async_copy(src.at[at], wide.at[k], sem_in.at[k]),
                    pltpu.make_async_copy(wide.at[k], dst.at[at], sem_out.at[k]),
                )
            )
    bring = pltpu.make_async_copy(fin, fin_v, sem_in.at[4])
    bring.start()
    for come, _ in moves:
        come.start()
    bring.wait()
    full[...] = fin_v[...].astype(f32)
    slot = lax.broadcasted_iota(jnp.int32, (2, LANES), 0)
    hot = [jnp.where(slot == bslot[k, section[0]], 1.0, 0.0) for k in range(2)]
    blocks = full.shape[2] // LANES

    def one(j, c):
        lanes = pl.ds(c * LANES, LANES)
        return sum(hot[k] * jnp.broadcast_to(full[k, pl.ds(j, 1), lanes], (2, LANES)) for k in range(2))

    for c in range(blocks):
        gains[:, pl.ds(c * LANES, LANES)] = one(31, c)

    for j in range(31):
        for c in range(blocks):
            taps[j, :, pl.ds(c * LANES, LANES)] = one(j, c)

    put = [
        pltpu.make_async_copy(taps, tap_out, sem_out.at[4]),
        pltpu.make_async_copy(gains, gain_out, sem_out.at[5]),
    ]
    for copy in put:
        copy.start()
    for come, go in moves:
        come.wait()
        go.start()
        put.append(go)
    for copy in put:
        copy.wait()


def finish(section, bslot, act, grad, fin):
    rows, width = act.shape
    vm = pltpu.VMEM
    dma = pltpu.SemaphoreType.DMA
    anywhere = pl.BlockSpec(memory_space=pl.ANY)
    scalars = pl.BlockSpec(memory_space=pltpu.SMEM)
    return pl.pallas_call(
        finish_body,
        out_shape=[
            jax.ShapeDtypeStruct((rows, width), bf16),
            jax.ShapeDtypeStruct((rows, width), bf16),
            jax.ShapeDtypeStruct((31, 2, width), f32),
            jax.ShapeDtypeStruct((2, width), f32),
        ],
        in_specs=[scalars] * 2 + [anywhere] * 3,
        out_specs=[anywhere] * 4,
        scratch_shapes=[
            vm((4, rows // 2, width), bf16),
            vm((2, 32, width), bf16),
            vm((2, 32, width), f32),
            vm((31, 2, width), f32),
            vm((2, width), f32),
            dma((5,)),
            dma((6,)),
        ],
        compiler_params=pltpu.CompilerParams(vmem_limit_bytes=56 << 20),
        name="finish",
    )(section, bslot, act, grad, fin)


def local_step(
    act_in,
    grad_in,
    saved_inputs,
    kernels,
    norm_gains,
    forward_lengths,
    backward_lengths,
    forward_slots,
    backward_slots,
):
    sections = lax.axis_size("section")
    shards = lax.axis_size("tm")
    s = lax.axis_index("section")
    act_out, grad_out, fin = relay(
        sections,
        shards,
        act_in[0],
        grad_in[0],
        saved_inputs[0],
        jnp.transpose(kernels[0], (1, 0, 2)),
        norm_gains[0],
        forward_lengths,
        backward_lengths,
        forward_slots.T,
        backward_slots.T,
    )
    act_out, grad_out, taps, gains = finish(s[None].astype(jnp.int32), backward_slots.T, act_out, grad_out, fin)
    return (act_out[None], grad_out[None], jnp.transpose(taps, (1, 0, 2))[None], gains[None])


def solution(mesh):
    in_specs = (
        P("section", "tm", None),
        P("section", "tm", None),
        P("section", None, "tm", None),
        P("section", None, None, None),
        P("section", None, None),
        P(),
        P(),
        P(),
        P(),
    )
    out_specs = (
        P("section", "tm", None),
        P("section", "tm", None),
        P("section", None, None, None),
        P("section", None, None),
    )
    return jax.shard_map(local_step, mesh=mesh, in_specs=in_specs, out_specs=out_specs, check_vma=False)
```

```python
import functools

import jax
import jax.numpy as jnp
from jax import lax
from jax.experimental import pallas as pl
from jax.experimental.pallas import tpu as pltpu
from jax.sharding import PartitionSpec as P

epsilon = 1e-05
MESH = pl.DeviceIdType.MESH
f32 = jnp.float32
bf16 = jnp.bfloat16
LANES = 128
PAD = 16


def row(ref, use, j, c):
    return jnp.broadcast_to(ref[use, pl.ds(j, 1), pl.ds(pl.multiple_of(c * LANES, LANES), LANES)], (8, LANES))


def conv_block(m_ref, k_ref, use, c, first, groups, flip):
    total = [None] * groups
    for b in range(8):
        taps = {}
        for a in range(4):
            o = 8 * a + b
            if o > 0:
                taps[a] = row(k_ref, use, 31 - o if flip else o - 1, c)
        for i in range(groups + 3):
            cells = m_ref[c, pl.ds(8 * (first + i) + b, 8), :]
            for a, tap in taps.items():
                r = i - a
                if 0 <= r < groups:
                    total[r] = tap * cells if total[r] is None else total[r] + tap * cells
    return total


def tap_block(m_ref, gm_ref, tap_ref, tick, c, groups):
    grads = [gm_ref[c, pl.ds(PAD + 8 * r, 8), :] for r in range(groups)]
    lanes = pl.ds(pl.multiple_of(c * LANES, LANES), LANES)
    for b in range(8):
        total = {}
        for i in range(groups + 3):
            cells = m_ref[c, pl.ds(8 * i + b, 8), :]
            for a in range(4):
                r = i - a
                if 8 * a + b > 0 and 0 <= r < groups:
                    total[a] = grads[r] * cells + total[a] if a in total else grads[r] * cells
        for a, value in total.items():
            tap_ref[tick, pl.ds(8 * a + b - 1, 1), lanes] = jnp.sum(value, axis=0, keepdims=True)


def body(
    sections,
    shards,
    act,
    grad,
    saved,
    kernels,
    gains,
    flen,
    blen,
    fslot,
    bslot,
    act_out,
    grad_out,
    fin,
    x_f,
    x_b,
    g_in,
    k_raw,
    gain_raw,
    k_ref,
    hx,
    m_f,
    m_b,
    gm,
    dref,
    scaled,
    mean_ref,
    inv_ref,
    a_ref,
    b_ref,
    y,
    gx,
    arrive_f,
    arrive_g,
    edge_f,
    gh_send,
    gh_recv,
    tap_ref,
    tap_bf,
    rs_buf,
    part,
    part_in,
    red,
    local_sem,
    hx_s,
    hx_r,
    y_s,
    y_r,
    e_s,
    e_r,
    g_s,
    g_r,
    gh_s,
    gh_r,
    rs_s,
    rs_r,
    pr_s,
    pr_r,
    ag_s,
    ag_r,
):
    s = lax.axis_index("section")
    t = lax.axis_index("tm")
    rows, width = act.shape
    blocks = width // LANES
    tiles = rows // 16
    quarter = width // 4
    quarter_blocks = blocks // 4
    band = rows // 4
    line = shards // 2
    own = width // line
    t_x, t_y = lax.rem(t, line), lax.div(t, line)
    after, before = lax.rem(s + 1, sections), lax.rem(s + sections - 1, sections)
    right, left = lax.rem(t + 1, shards), lax.rem(t + shards - 1, shards)
    base = t * rows
    outer = ((0, band // 8), (3 * band // 8, band // 8))
    inner = ((band // 8, band // 4),)

    barrier = pltpu.get_barrier_semaphore()
    peers = [(after, t), (before, t), (after, left), (after, right), (before, left), (before, right)]
    peers += [(s, lax.rem(t + d, shards)) for d in range(1, shards)]
    for peer in peers:
        pl.semaphore_signal(barrier, inc=1, device_id=peer, device_id_type=MESH)

    def local(src, dst, n):
        return pltpu.make_async_copy(src, dst, local_sem.at[n])

    loads = [
        local(kernels, k_raw, 0),
        local(gains, gain_raw, 1),
        local(saved.at[0], x_b.at[0], 2),
        local(act, x_f, 3),
        local(saved.at[1], x_b.at[1], 4),
        local(grad, g_in, 5),
    ]
    for copy in loads:
        copy.start()

    sent = []

    def remote(src, dst, send, recv, peer):
        return pltpu.make_async_remote_copy(
            src_ref=src, dst_ref=dst, send_sem=send, recv_sem=recv, device_id=peer, device_id_type=MESH
        )

    def launch(copy):
        copy.start()
        sent.append(copy)
        return copy

    def lanes_of(c):
        return pl.ds(pl.multiple_of(c * LANES, LANES), LANES)

    def twice(value):
        return jnp.concatenate([value, value], axis=0)

    f_len = [flen[lax.rem(s + sections - k, sections)] for k in range(2)]
    b_len = [blen[lax.rem(s + k, sections)] for k in range(2)]
    slots = [fslot[0, s], fslot[1, s], bslot[0, s], bslot[1, s]]

    def pick(use):
        one = slots[use].astype(f32)
        zero = 1.0 - one
        pair = gain_raw[...].astype(f32)
        k_ref[use, pl.ds(31, 1), :] = pair[0:1] * zero + pair[1:2] * one

        for j in range(31):
            pair = k_raw[j].astype(f32)
            k_ref[use, pl.ds(j, 1), :] = pair[0:1] * zero + pair[1:2] * one

    def normalize(load, count, frames, at, length, use, m_ref, keep=None):
        zeros = [jnp.zeros((16, LANES), f32)] * count

        def sums(c, totals):
            return [total + load(n, c) for n, total in enumerate(totals)]

        totals = lax.fori_loop(0, blocks, sums, zeros, unroll=4)
        means = [
            jnp.broadcast_to(jnp.sum(total, axis=1, keepdims=True) * (1.0 / width), (16, LANES)) for total in totals
        ]

        def squares(c, totals):
            out = []
            for n, total in enumerate(totals):
                center = load(n, c) - means[n]
                out.append(total + center * center)
            return out

        totals = lax.fori_loop(0, blocks, squares, zeros, unroll=4)
        scales = []
        for n, total in enumerate(totals):
            var = jnp.sum(total, axis=1, keepdims=True) * (1.0 / width)
            inverse = jnp.broadcast_to(lax.rsqrt(var + epsilon), (16, LANES))
            if keep is not None:
                mean_ref[keep, pl.ds(16 * n, 16), :] = means[n]
                inv_ref[keep, pl.ds(16 * n, 16), :] = inverse
            ids = frames[n] + lax.broadcasted_iota(jnp.int32, (16, LANES), 0)
            scales.append(jnp.where((ids >= 0) & (ids < length), inverse, 0.0))

        def write(c, _):
            gain = twice(row(k_ref, use, 31, c))
            for n in range(count):
                m_ref[c, pl.ds(at[n], 16), :] = (load(n, c) - means[n]) * scales[n] * gain
            return 0

        lax.fori_loop(0, blocks, write, 0, unroll=2)

    def norm_own(x_ref, length, use, m_ref, keep=None):
        normalize(
            lambda n, c: x_ref[pl.ds(16 * n, 16), lanes_of(c)].astype(f32),
            tiles,
            [base + 16 * n for n in range(tiles)],
            [PAD + 16 * n for n in range(tiles)],
            length,
            use,
            m_ref,
            keep,
        )

    def norm_edges(h_ref, length, use, m_ref):
        normalize(
            lambda n, c: h_ref[n, :, lanes_of(c)].astype(f32),
            2,
            [base - PAD, base + rows],
            [0, rows + PAD],
            length,
            use,
            m_ref,
        )

    pl.semaphore_wait(barrier, len(peers))

    halos = {}
    for n, ref in ((1, saved.at[0]), (0, act), (2, saved.at[1])):
        halos[n] = []
        for side, peer in ((1, left), (0, right)):
            edge = pl.ds(0, 16) if side == 1 else pl.ds(rows - 16, 16)
            halos[n].append(
                launch(remote(ref.at[edge], hx.at[n, side], hx_s.at[n, side], hx_r.at[n, side], (s, peer)))
            )

    loads[0].wait()
    loads[1].wait()
    pick(2)
    loads[2].wait()
    norm_own(x_b.at[0], b_len[0], 2, m_b.at[0], 0)
    loads[3].wait()
    pick(0)
    norm_own(x_f, f_len[0], 0, m_f)
    loads[4].wait()
    pick(3)
    norm_own(x_b.at[1], b_len[1], 3, m_b.at[1], 1)

    def forward(tick, x_ref, dst):
        copies = [
            remote(
                y.at[tick, :, pl.ds(q * quarter, quarter)],
                dst.at[:, pl.ds(q * quarter, quarter)],
                y_s.at[tick, q],
                y_r.at[tick, q],
                (after, t),
            )
            for q in range(4)
        ]

        @pl.loop(0, blocks)
        def _(c):
            total = conv_block(m_f, k_ref, tick, c, 0, 2 * tiles, False)
            for r in range(tiles):
                conv = jnp.concatenate(total[2 * r : 2 * r + 2], axis=0)
                x = x_ref[pl.ds(16 * r, 16), lanes_of(c)].astype(f32)
                y[tick, pl.ds(16 * r, 16), lanes_of(c)] = (x + conv * jax.nn.sigmoid(conv)).astype(bf16)
            for q in range(4):

                @pl.when(c == (q + 1) * quarter_blocks - 1)
                def _():
                    copies[q].start()

        sent.extend(copies)
        return copies

    def slope(conv):
        gate = jax.nn.sigmoid(conv)
        return gate * (1.0 + conv * (1.0 - gate))

    def put_mixed(tick, c, r, value):
        gm[c, pl.ds(PAD + 16 * r, 16), :] = value
        if r == 0:
            gh_send[tick, 1, :, lanes_of(c)] = value.astype(bf16)
        if r == tiles - 1:
            gh_send[tick, 0, :, lanes_of(c)] = value.astype(bf16)

    def send_mixed(tick):
        return [
            launch(
                remote(
                    gh_send.at[tick, side],
                    gh_recv.at[tick, side],
                    gh_s.at[tick, side],
                    gh_r.at[tick, side],
                    (s, peer),
                )
            )
            for side, peer in ((1, left), (0, right))
        ]

    def taps(tick):
        @pl.loop(0, blocks)
        def _(c):
            tap_block(m_b.at[tick], gm, tap_ref, tick, c, 2 * tiles)

        tap_bf[tick] = tap_ref[tick].astype(bf16)

    def mixed_edges(tick, copies):
        for copy in copies:
            copy.wait_recv()
        inside = (jnp.where(t > 0, 1.0, 0.0), jnp.where(t < shards - 1, 1.0, 0.0))

        @pl.loop(0, blocks)
        def _(c):
            for side in range(2):
                gm[c, pl.ds(side * (rows + PAD), 16), :] = gh_recv[tick, side, :, lanes_of(c)].astype(f32) * inside[side]

    def normed(tick, r, c):
        x = x_b[tick, pl.ds(r, 16), lanes_of(c)].astype(f32)
        return (x - mean_ref[tick, pl.ds(r, 16), :]) * inv_ref[tick, pl.ds(r, 16), :]

    def input_grad(tick, g_ref, dst):
        use = 2 + tick
        a_ref[...] = jnp.zeros_like(a_ref)
        b_ref[...] = jnp.zeros_like(b_ref)
        copies = {}
        for turn, (segments, bands) in enumerate(((outer, (0, 3)), (inner, (1, 2)))):

            @pl.loop(0, blocks)
            def _(c):
                gain = twice(row(k_ref, use, 31, c))
                ids = base + lax.broadcasted_iota(jnp.int32, (16, LANES), 0)
                term = None
                for first, groups in segments:
                    total = conv_block(gm, k_ref, use, c, first, groups, True)
                    for n in range(groups // 2):
                        r = 8 * first + 16 * n
                        value = jnp.concatenate(total[2 * n : 2 * n + 2], axis=0)
                        value = jnp.where(ids < b_len[tick] - r, value, 0.0)
                        norm = normed(tick, r, c)
                        part_term = value * norm
                        term = part_term if term is None else term + part_term
                        value = value * gain
                        at = pl.ds(r, 16)
                        scaled[c, at, :] = value
                        a_ref[at, :] += value
                        b_ref[at, :] += value * norm
                total_term = jnp.sum(term, axis=0, keepdims=True)
                if turn > 0:
                    total_term = total_term + tap_ref[tick, pl.ds(31, 1), lanes_of(c)]
                tap_ref[tick, pl.ds(31, 1), lanes_of(c)] = total_term

            starts = [q * band + 16 * n for q in bands for n in range(band // 16)]
            fixed = []
            for r in starts:
                at = pl.ds(r, 16)
                mean_a = jnp.broadcast_to(jnp.sum(a_ref[at, :], axis=1, keepdims=True) * (1.0 / width), (16, LANES))
                mean_b = jnp.broadcast_to(jnp.sum(b_ref[at, :], axis=1, keepdims=True) * (1.0 / width), (16, LANES))
                fixed.append((mean_a, mean_b))
            for (mean_a, mean_b), r in zip(fixed, starts):
                a_ref[pl.ds(r, 16), :] = mean_a
                b_ref[pl.ds(r, 16), :] = mean_b
            for q in bands:
                mine = [q * band + 16 * n for n in range(band // 16)]
                held = [
                    [ref[pl.ds(r, 16), :] for ref in (a_ref, b_ref, mean_ref.at[tick], inv_ref.at[tick])] for r in mine
                ]

                def write(c, _):
                    for r, (mean_a, mean_b, mean, inverse) in zip(mine, held):
                        at = pl.ds(r, 16)
                        norm = (x_b[tick, at, lanes_of(c)].astype(f32) - mean) * inverse
                        value = (scaled[c, at, :] - mean_a - norm * mean_b) * inverse
                        gx[tick, at, lanes_of(c)] = (g_ref[at, lanes_of(c)].astype(f32) + value).astype(bf16)
                    return 0

                lax.fori_loop(0, blocks, write, 0, unroll=2)
                copies[q] = launch(
                    remote(
                        gx.at[tick, pl.ds(q * band, band)],
                        dst.at[pl.ds(q * band, band)],
                        g_s.at[tick, q],
                        g_r.at[tick, q],
                        (before, t),
                    )
                )
        return copies

    def lane_part(n):
        return pl.ds(pl.multiple_of(n * own, LANES), own)

    def scatter(tick):
        for d in range(1, line):
            peer = lax.rem(t_x + d, line)
            launch(
                remote(
                    tap_bf.at[tick, :, lane_part(peer)],
                    rs_buf.at[tick, t_x],
                    rs_s.at[tick, d],
                    rs_r.at[tick, t_x],
                    (s, t_y * line + peer),
                )
            )

    def exchange(tick):
        value = tap_ref[tick, :, lane_part(t_x)]
        for d in range(1, line):
            peer = lax.rem(t_x + d, line)
            remote(
                tap_bf.at[tick, :, lane_part(peer)],
                rs_buf.at[tick, peer],
                rs_s.at[tick, d],
                rs_r.at[tick, peer],
                (s, t_y * line + peer),
            ).wait_recv()
            value = value + rs_buf[tick, peer].astype(f32)
        part[tick] = value.astype(bf16)
        return launch(
            remote(part.at[tick], part_in.at[tick], pr_s.at[tick], pr_r.at[tick], (s, (1 - t_y) * line + t_x))
        )

    def gather(tick, swap):
        swap.wait_recv()
        red[tick] = (part[tick].astype(f32) + part_in[tick].astype(f32)).astype(bf16)
        keep = local(red.at[tick], fin.at[tick, :, lane_part(t_x)], 6 + tick)
        keep.start()
        loads.append(keep)
        for d in range(1, line):
            launch(
                remote(
                    red.at[tick],
                    fin.at[tick, :, lane_part(t_x)],
                    ag_s.at[tick, d],
                    ag_r.at[tick, t_x],
                    (s, t_y * line + lax.rem(t_x + d, line)),
                )
            )

    def gathered(tick):
        for d in range(1, line):
            peer = lax.rem(t_x + d, line)
            remote(
                red.at[tick],
                fin.at[tick, :, lane_part(peer)],
                ag_s.at[tick, d],
                ag_r.at[tick, peer],
                (s, t_y * line + peer),
            ).wait_recv()

    for copy in halos[1]:
        copy.wait_recv()
    norm_edges(hx.at[1], b_len[0], 2, m_b.at[0])
    loads[5].wait()

    for segments in (outer, inner):

        @pl.loop(0, blocks)
        def _(c):
            for first, groups in segments:
                total = conv_block(m_b.at[0], k_ref, 2, c, first, groups, False)
                for n in range(groups // 2):
                    r = first // 2 + n
                    conv = jnp.concatenate(total[2 * n : 2 * n + 2], axis=0)
                    put_mixed(0, c, r, g_in[pl.ds(16 * r, 16), lanes_of(c)].astype(f32) * slope(conv))

        if segments is outer:
            mixed = send_mixed(0)

    for copy in halos[0]:
        copy.wait_recv()
    norm_edges(hx.at[0], f_len[0], 0, m_f)
    ahead = forward(0, x_f, arrive_f)
    edges = []
    for side, peer in ((1, left), (0, right)):
        edge = pl.ds(0, 16) if side == 1 else pl.ds(rows - 16, 16)
        edges.append(launch(remote(y.at[0, edge], edge_f.at[side], e_s.at[side], e_r.at[side], (after, peer))))
    mixed_edges(0, mixed)
    behind = input_grad(0, g_in, arrive_g)
    taps(0)
    scatter(0)

    for copy in halos[2]:
        copy.wait_recv()
    norm_edges(hx.at[2], b_len[1], 3, m_b.at[1])

    @pl.loop(0, blocks)
    def _(c):
        total = conv_block(m_b.at[1], k_ref, 3, c, 0, 2 * tiles, False)
        for r in range(tiles):
            conv = jnp.concatenate(total[2 * r : 2 * r + 2], axis=0)
            dref[c, pl.ds(16 * r, 16), :] = slope(conv)

    pick(1)
    swap = exchange(0)

    def mix_bands(bands):
        for q in bands:
            behind[q].wait_recv()

        @pl.loop(0, blocks)
        def _(c):
            for q in bands:
                for r in range(q * band // 16, (q + 1) * band // 16):
                    at = pl.ds(16 * r, 16)
                    put_mixed(1, c, r, arrive_g[at, lanes_of(c)].astype(f32) * dref[c, at, :])

    mix_bands((0, 3))
    mixed = send_mixed(1)
    gather(0, swap)
    for copy in ahead + edges:
        copy.wait_recv()
    norm_own(arrive_f, f_len[1], 1, m_f)
    norm_edges(edge_f, f_len[1], 1, m_f)
    ahead = forward(1, arrive_f, act_out)
    mix_bands((1, 2))
    mixed_edges(1, mixed)
    behind = input_grad(1, arrive_g, grad_out)
    taps(1)
    scatter(1)
    swap = exchange(1)
    gather(1, swap)
    gathered(0)
    gathered(1)
    for copy in ahead + list(behind.values()):
        copy.wait_recv()
    for copy in sent:
        copy.wait_send()
    for copy in loads[6:]:
        copy.wait()


def relay(sections, shards, act, grad, saved, kernels, gains, flen, blen, fslot, bslot):
    rows, width = act.shape
    blocks = width // LANES
    line = shards // 2
    own = width // line
    vm = pltpu.VMEM
    dma = pltpu.SemaphoreType.DMA
    padded_rows = rows + 2 * PAD
    anywhere = pl.BlockSpec(memory_space=pl.ANY)
    scalars = pl.BlockSpec(memory_space=pltpu.SMEM)
    return pl.pallas_call(
        functools.partial(body, sections, shards),
        out_shape=[
            jax.ShapeDtypeStruct((rows, width), bf16),
            jax.ShapeDtypeStruct((rows, width), bf16),
            jax.ShapeDtypeStruct((2, 32, width), bf16),
        ],
        in_specs=[anywhere] * 5 + [scalars] * 4,
        out_specs=[anywhere] * 3,
        scratch_shapes=[
            vm((rows, width), bf16),
            vm((2, rows, width), bf16),
            vm((rows, width), bf16),
            vm((31, 2, width), bf16),
            vm((2, width), bf16),
            vm((4, 32, width), f32),
            vm((3, 2, 16, width), bf16),
            vm((blocks, padded_rows, LANES), f32),
            vm((2, blocks, padded_rows, LANES), f32),
            vm((blocks, padded_rows, LANES), f32),
            vm((blocks, rows, LANES), f32),
            vm((blocks, rows, LANES), f32),
            vm((2, rows, LANES), f32),
            vm((2, rows, LANES), f32),
            vm((rows, LANES), f32),
            vm((rows, LANES), f32),
            vm((2, rows, width), bf16),
            vm((2, rows, width), bf16),
            vm((rows, width), bf16),
            vm((rows, width), bf16),
            vm((2, 16, width), bf16),
            vm((2, 2, 16, width), bf16),
            vm((2, 2, 16, width), bf16),
            vm((2, 32, width), f32),
            vm((2, 32, width), bf16),
            vm((2, line, 32, own), bf16),
            vm((2, 32, own), bf16),
            vm((2, 32, own), bf16),
            vm((2, 32, own), bf16),
            dma((8,)),
            dma((3, 2)),
            dma((3, 2)),
            dma((2, 4)),
            dma((2, 4)),
            dma((2,)),
            dma((2,)),
            dma((2, 4)),
            dma((2, 4)),
            dma((2, 2)),
            dma((2, 2)),
            dma((2, line)),
            dma((2, line)),
            dma((2,)),
            dma((2,)),
            dma((2, line)),
            dma((2, line)),
        ],
        compiler_params=pltpu.CompilerParams(collective_id=0, has_side_effects=True, vmem_limit_bytes=56 << 20),
        name="relay",
    )(act, grad, saved, kernels, gains, flen, blen, fslot, bslot)


def finish_body(section, bslot, act, grad, fin, act_out, grad_out, tap_out, gain_out, wide, fin_v, full, taps, gains, sem_in, sem_out):
    rows = act.shape[0]
    half = rows // 2
    moves = []
    for n, (src, dst) in enumerate(((act, act_out), (grad, grad_out))):
        for h in range(2):
            at = pl.ds(h * half, half)
            k = 2 * n + h
            moves.append(
                (
                    pltpu.make_async_copy(src.at[at], wide.at[k], sem_in.at[k]),
                    pltpu.make_async_copy(wide.at[k], dst.at[at], sem_out.at[k]),
                )
            )
    bring = pltpu.make_async_copy(fin, fin_v, sem_in.at[4])
    bring.start()
    for come, _ in moves:
        come.start()
    for come, go in moves:
        come.wait()
        go.start()
    bring.wait()
    full[...] = fin_v[...].astype(f32)
    slot = lax.broadcasted_iota(jnp.int32, (2, LANES), 0)
    hot = [jnp.where(slot == bslot[k, section[0]], 1.0, 0.0) for k in range(2)]
    blocks = full.shape[2] // LANES

    def one(j, c):
        lanes = pl.ds(c * LANES, LANES)
        return sum(hot[k] * jnp.broadcast_to(full[k, pl.ds(j, 1), lanes], (2, LANES)) for k in range(2))

    put = []
    for n, (first, count) in enumerate(((0, 8), (8, 8), (16, 8), (24, 7))):
        for j in range(first, first + count):
            for c in range(blocks):
                taps[j, :, pl.ds(c * LANES, LANES)] = one(j, c)
        at = pl.ds(first, count)
        put.append(pltpu.make_async_copy(taps.at[at], tap_out.at[at], sem_out.at[4 + n]))
        put[-1].start()
    for c in range(blocks):
        gains[:, pl.ds(c * LANES, LANES)] = one(31, c)
    put.append(pltpu.make_async_copy(gains, gain_out, sem_out.at[8]))
    put[-1].start()
    for copy in put + [go for _, go in moves]:
        copy.wait()


def finish(section, bslot, act, grad, fin):
    rows, width = act.shape
    vm = pltpu.VMEM
    dma = pltpu.SemaphoreType.DMA
    anywhere = pl.BlockSpec(memory_space=pl.ANY)
    scalars = pl.BlockSpec(memory_space=pltpu.SMEM)
    return pl.pallas_call(
        finish_body,
        out_shape=[
            jax.ShapeDtypeStruct((rows, width), bf16),
            jax.ShapeDtypeStruct((rows, width), bf16),
            jax.ShapeDtypeStruct((31, 2, width), f32),
            jax.ShapeDtypeStruct((2, width), f32),
        ],
        in_specs=[scalars] * 2 + [anywhere] * 3,
        out_specs=[anywhere] * 4,
        scratch_shapes=[
            vm((4, rows // 2, width), bf16),
            vm((2, 32, width), bf16),
            vm((2, 32, width), f32),
            vm((31, 2, width), f32),
            vm((2, width), f32),
            dma((5,)),
            dma((9,)),
        ],
        compiler_params=pltpu.CompilerParams(vmem_limit_bytes=56 << 20),
        name="finish",
    )(section, bslot, act, grad, fin)


def local_step(
    act_in,
    grad_in,
    saved_inputs,
    kernels,
    norm_gains,
    forward_lengths,
    backward_lengths,
    forward_slots,
    backward_slots,
):
    sections = lax.axis_size("section")
    shards = lax.axis_size("tm")
    s = lax.axis_index("section")
    act_out, grad_out, fin = relay(
        sections,
        shards,
        act_in[0],
        grad_in[0],
        saved_inputs[0],
        jnp.transpose(kernels[0], (1, 0, 2)),
        norm_gains[0],
        forward_lengths,
        backward_lengths,
        forward_slots.T,
        backward_slots.T,
    )
    act_out, grad_out, taps, gains = finish(s[None].astype(jnp.int32), backward_slots.T, act_out, grad_out, fin)
    return (act_out[None], grad_out[None], jnp.transpose(taps, (1, 0, 2))[None], gains[None])


def solution(mesh):
    in_specs = (
        P("section", "tm", None),
        P("section", "tm", None),
        P("section", None, "tm", None),
        P("section", None, None, None),
        P("section", None, None),
        P(),
        P(),
        P(),
        P(),
    )
    out_specs = (
        P("section", "tm", None),
        P("section", "tm", None),
        P("section", None, None, None),
        P("section", None, None),
    )
    return jax.shard_map(local_step, mesh=mesh, in_specs=in_specs, out_specs=out_specs, check_vma=False)
```
